32 devices in a mesh: blk: 8 (over z, x), rep: 4 (over y, core).
Axes of the slice: x: 2, y: 2, z: 4, core: 2. Of those that a mesh axis runs over, the one named last changes fastest.
Arguments:
- features: bfloat16 [4096, 512], P('blk', 'rep'), may hold values from -6 to 6
- row_target: int32 [4096], P('blk'), may hold values from 0 to 4095, as said below
- tile_values: bfloat16 [8, 8, 4, 128, 128], P('blk'), may hold values from -0.25 to 0.25
- tile_rows: int32 [8, 8, 4], P('blk'), may hold values from 0 to 3, as said below
- tile_cols: int32 [8, 8, 4], P('blk'), may hold values from 0 to 3, as said below
- tile_counts: int32 [8, 8], P('blk'), may hold values from 0 to 4, as said below
- weight: bfloat16 [512, 512], P('rep'), may hold values from -0.25 to 0.25
- layer_bias: float32 [512], replicated, may hold values from -3 to 3
- out_grad: bfloat16 [4096, 512], P('blk'), may hold values from -0.75 to 0.75
Outputs:
- output: bfloat16 [4096, 512], P(('blk', 'rep'))
- weight_grad: float32 [512, 512], P('rep')
- bias_grad: float32 [512], replicated
- feature_grad: bfloat16 [4096, 512], P('blk', 'rep')
The draws below stay inside these ranges and needn't reach their ends.
Inputs may be any that keep to these rules, and one draw needn't show every extreme that they name: `row_target`: a permutation of the 4096 rows; the rows of one loader block of 512 rows bound for one partition number at most 128, and this many in every draw. `tile_rows`: within one pair of partitions the live slots name distinct tile positions. `tile_cols`: within one pair of partitions the live slots name distinct tile positions. `tile_counts`: every pair of a partition with itself has all 4 slots live; each row partition has live slots with exactly 6 other partitions, and none with the rest.
All inputs are finite; a program needn't handle non-finite values.
Results may differ from the reference program's by a relative error of at most 0.0061.
Values may be sent and summed in bfloat16 or wider, within the bound.
No kernel may reach another device: no remote copies, remote signals or barrier semaphores. Data moves between devices by JAX's collectives and lax.ppermute only.
A program may use at most 128 MiB of HBM per device.

```python
import jax
import jax.numpy as jnp
from jax import lax

F = 512
TILE = 128
SLOTS = 4
PARTNERS = 6
ROWS = 512
NODES = 4096
REACH = 608
N_BLK = 8


def draw_row_target(key, part):
    baseline = ROWS // N_BLK
    quarter = N_BLK // 4
    first_key, second_key, third_key = jax.random.split(key, 3)
    offsets_order = jax.random.permutation(first_key, N_BLK)
    loads = jnp.full((N_BLK,), baseline, jnp.int32)
    loads = loads.at[offsets_order[:quarter]].set(2 * baseline)
    loads = loads.at[offsets_order[quarter:2 * quarter]].set(0)
    sources = jnp.arange(N_BLK, dtype=jnp.int32)
    counts = loads[(sources[None, :] - sources[:, None]) % N_BLK]
    arrival = jnp.cumsum(counts, axis=0) - counts
    starting = jnp.cumsum(counts, axis=1) - counts
    inner = jax.vmap(lambda single: jax.random.permutation(single, ROWS).astype(jnp.int32))(jax.random.split(second_key, N_BLK))
    shuffle = jax.vmap(lambda single: jax.random.permutation(single, ROWS).astype(jnp.int32))(jax.random.split(third_key, N_BLK))
    positions = jnp.arange(ROWS, dtype=jnp.int32)

    def one_source(source, count_row, start_row, order_row):
        target = jnp.repeat(sources, count_row, total_repeat_length=ROWS)
        ranked = positions - start_row[target]
        landing = arrival[source, target] + ranked
        value = target * ROWS + inner[target, landing]
        return (source * ROWS + order_row, value)
    where_from, value = jax.vmap(one_source)(sources, counts, starting, shuffle)
    return jnp.zeros((N_BLK * ROWS,), jnp.int32).at[where_from.reshape(-1)].set(value.reshape(-1))


def tile_places(key):
    folded = jax.random.fold_in(key, 11)
    row_tiles = ROWS // TILE
    keys = jax.random.split(folded, N_BLK * N_BLK)
    picks = jax.vmap(lambda single: jax.random.permutation(single, row_tiles * row_tiles)[:SLOTS])(keys)
    return (picks.reshape(N_BLK, N_BLK, SLOTS).astype(jnp.int32), row_tiles)


def draw_tile_rows(key, part):
    picks, row_tiles = tile_places(key)
    return picks // row_tiles


def draw_tile_cols(key, part):
    picks, row_tiles = tile_places(key)
    return picks % row_tiles


def draw_tile_counts(key, part):
    first_key, second_key = jax.random.split(key, 2)
    row_keys = jax.random.split(first_key, N_BLK)
    offsets = jax.vmap(lambda single: jax.random.permutation(single, N_BLK - 1)[:PARTNERS].astype(jnp.int32))(row_keys)
    diagonal = jnp.arange(N_BLK, dtype=jnp.int32)
    partner_cols = (diagonal[:, None] + 1 + offsets) % N_BLK
    levels = jax.random.randint(second_key, (N_BLK, PARTNERS), 1, SLOTS + 1).astype(jnp.int32)
    counts = jnp.zeros((N_BLK, N_BLK), jnp.int32)
    counts = counts.at[diagonal[:, None], partner_cols].set(levels)
    counts = counts.at[diagonal, diagonal].set(SLOTS)
    return counts.astype(jnp.int32)


def shard_levels(key, shape, cuts, low, high):
    loudness, own = 1.0, jax.random.fold_in(key, 6)
    for dim, parts in cuts:
        steps = jnp.exp(jax.random.uniform(jax.random.fold_in(own, dim), (parts,), jnp.float32, low / len(cuts), high / len(cuts)))
        loudness = loudness * jnp.repeat(steps, shape[dim] // parts).reshape([-1 if axis == dim else 1 for axis in range(len(shape))])
    return loudness


def noise(own_key, extent, deviation, bound, cuts=(), kind=jnp.bfloat16):
    loudness = shard_levels(own_key, extent, cuts, -0.22, 0.18) if cuts else 1.0
    array = jax.random.normal(own_key, extent, jnp.float32) * deviation * loudness
    return jnp.minimum(jnp.maximum(array, -bound), bound).astype(kind)


def setup_inputs(seed: int = 0) -> dict:
    splits = jax.random.split(jax.random.key(seed), 10)
    features = noise(splits[0], (NODES, F), 1.0, 6.0, ((0, 8), (1, 4)))
    row_target = draw_row_target(jax.random.fold_in(splits[9], 71), 0)
    tile_values = noise(splits[2], (N_BLK, N_BLK, SLOTS, TILE, TILE), REACH ** -0.5, 0.25, ((0, 8),))
    tile_rows = draw_tile_rows(jax.random.fold_in(splits[9], 71), 0)
    tile_cols = draw_tile_cols(jax.random.fold_in(splits[9], 71), 0)
    tile_counts = draw_tile_counts(jax.random.fold_in(splits[9], 71), 0)
    weight = noise(splits[6], (F, F), F ** -0.5, 0.25, ((0, 4),))
    layer_bias = noise(splits[7], (F,), 0.5, 3.0, (), jnp.float32)
    out_grad = noise(splits[8], (NODES, F), 0.125, 0.75, ((0, 8),))
    return dict(features=features, row_target=row_target, tile_values=tile_values, tile_rows=tile_rows, tile_cols=tile_cols, tile_counts=tile_counts, weight=weight, layer_bias=layer_bias, out_grad=out_grad)


def reference(features, row_target, tile_values, tile_rows, tile_cols, tile_counts, weight, layer_bias, out_grad):
    row_tiles = ROWS // TILE
    node_count = features.shape[0]
    regrouped = jnp.zeros_like(features).at[row_target].set(features)
    reg_tiles = regrouped.astype(jnp.float32).reshape(node_count // TILE, TILE, F)
    slot_ids = jnp.arange(SLOTS, dtype=jnp.int32)
    blocks = jnp.arange(N_BLK, dtype=jnp.int32)
    tile_ids = jnp.arange(row_tiles, dtype=jnp.int32)

    def row_part(part):
        values = tile_values[part].astype(jnp.float32)
        live = slot_ids[None, :] < tile_counts[part][:, None]
        column = blocks[:, None] * row_tiles + tile_cols[part]
        inputs = reg_tiles[column]
        product = jnp.einsum("qsij,qsjf->qsif", values, inputs, precision=lax.Precision.HIGHEST)
        place = ((tile_rows[part][..., None] == tile_ids) & live[..., None]).astype(jnp.float32)
        return jnp.einsum("qsr,qsif->rif", place, product, precision=lax.Precision.HIGHEST).reshape(ROWS, F)

    mixed = lax.map(row_part, blocks).reshape(node_count, F).astype(jnp.bfloat16)
    pre = jnp.dot(mixed, weight, preferred_element_type=jnp.float32) + layer_bias
    sigma = jax.nn.sigmoid(pre)
    output = (pre * sigma).astype(jnp.bfloat16)
    pre_grad = (out_grad.astype(jnp.float32) * sigma * (1.0 + pre * (1.0 - sigma))).astype(jnp.bfloat16)
    bias_grad = jnp.sum(pre_grad.astype(jnp.float32), axis=0)
    weight_grad = jnp.dot(mixed.T, pre_grad, preferred_element_type=jnp.float32)
    mixed_grad = jnp.dot(pre_grad, weight.T, preferred_element_type=jnp.float32).astype(jnp.bfloat16)
    grad_tiles = mixed_grad.astype(jnp.float32).reshape(node_count // TILE, TILE, F)

    def col_part(part):
        values = tile_values[:, part].astype(jnp.float32)
        live = slot_ids[None, :] < tile_counts[:, part][:, None]
        source = blocks[:, None] * row_tiles + tile_rows[:, part]
        inputs = grad_tiles[source]
        product = jnp.einsum("psij,psif->psjf", values, inputs, precision=lax.Precision.HIGHEST)
        place = ((tile_cols[:, part][..., None] == tile_ids) & live[..., None]).astype(jnp.float32)
        return jnp.einsum("psr,psjf->rjf", place, product, precision=lax.Precision.HIGHEST).reshape(ROWS, F)

    feature_grad = lax.map(col_part, blocks).reshape(node_count, F).astype(jnp.bfloat16)
    return output, weight_grad, bias_grad, feature_grad
```

```python
import functools

import jax
import jax.numpy as jnp
from jax import lax
from jax.experimental import pallas as pl
from jax.experimental.pallas import tpu as pltpu
from jax.sharding import PartitionSpec as P


F32 = jnp.float32
BF16 = jnp.bfloat16
I32 = jnp.int32
DIGIT = 256
PACK = 16
VMEM_BUDGET = 24 * 1024 * 1024
VMEM_LIMIT = 32 * 1024 * 1024
VM = pl.BlockSpec(memory_space=pltpu.VMEM)
SM = pl.BlockSpec(memory_space=pltpu.SMEM)


def call(body, out_shape, in_specs, scratch=(), flops=0, moved=0, name=None):
    many = isinstance(out_shape, (list, tuple))
    return pl.pallas_call(
        body,
        out_shape=out_shape,
        in_specs=in_specs,
        out_specs=[VM] * len(out_shape) if many else VM,
        scratch_shapes=list(scratch),
        compiler_params=pltpu.CompilerParams(vmem_limit_bytes=VMEM_LIMIT),
        cost_estimate=pl.CostEstimate(flops=flops, bytes_accessed=moved, transcendentals=0),
        name=name,
    )


def swap(x, axis, offset):
    count = lax.axis_size(axis)
    return lax.ppermute(x, axis, [(i, i ^ offset) for i in range(count)])


def densify_body(rows_ref, cols_ref, counts_ref, values_ref, dense_ref):
    spans, slots, tile, _ = values_ref.shape
    per_span = dense_ref.shape[1] // (spans * tile)
    dense_ref[...] = jnp.zeros_like(dense_ref)
    for q in range(spans):
        for s in range(slots):

            @pl.when(s < counts_ref[q])
            def _(q=q, s=s):
                top = pl.multiple_of(rows_ref[q * slots + s] * tile, tile)
                left = pl.multiple_of((q * per_span + cols_ref[q * slots + s]) * tile, tile)
                dense_ref[pl.ds(top, tile), pl.ds(left, tile)] = values_ref[q, s]


def targets_of(block_ref, rows):
    lanes = block_ref.shape[1]
    lines = rows // lanes
    digits = block_ref[rows : rows + PACK, :].astype(F32)
    found = digits[0:lines] * DIGIT + digits[lines : 2 * lines]
    found = found.astype(I32)
    return jnp.concatenate([found[i : i + 1] for i in range(lines)], axis=1)


def regroup_span(block_refs, targets, span, rows):
    total = None
    spots = lax.broadcasted_iota(I32, (rows, rows), 0) + span * rows
    for ref, where in zip(block_refs, targets):
        pick = jnp.where(spots == where, 1.0, 0.0).astype(BF16)
        term = jnp.dot(pick, ref[0:rows, :], preferred_element_type=F32)
        total = term if total is None else total + term
    return total


def regroup_body(spans, rows, *refs):
    *block_refs, out_ref = refs
    targets = [targets_of(ref, rows) for ref in block_refs]

    def step(span, carry):
        at = pl.multiple_of(span * rows, rows)
        out_ref[pl.ds(at, rows), :] = regroup_span(block_refs, targets, span, rows).astype(BF16)
        return carry

    lax.fori_loop(0, spans, step, 0)


def mix_body(spans, rows, *refs):
    *block_refs, early_ref, dense_ref, out_ref, total_ref = refs
    targets = [targets_of(ref, rows) for ref in block_refs]
    total_ref[...] = jnp.zeros_like(total_ref)

    def step(span, carry):
        at = pl.multiple_of(span * rows, rows)
        late = regroup_span(block_refs, targets, span, rows)
        placed = (late + early_ref[pl.ds(at, rows), :].astype(F32)).astype(BF16)
        total_ref[...] += jnp.dot(
            dense_ref[:, pl.ds(at, rows)], placed, preferred_element_type=F32
        )
        return carry

    lax.fori_loop(0, spans, step, 0)
    out_ref[...] = total_ref[...].astype(BF16)


def layer_body(members, me_ref, *refs):
    mixed_refs = refs[:members]
    weight_refs = refs[members : 2 * members]
    bias_ref, cotangent_ref, out_ref, send_ref, grad_ref, mixed_all, weight_all, pre_grad = refs[
        2 * members :
    ]
    rows, share = mixed_refs[0].shape
    width = weight_refs[0].shape[1]
    me = me_ref[0]
    for k in range(members):
        at = pl.multiple_of((me ^ k) * share, share)
        mixed_all[:, pl.ds(at, share)] = mixed_refs[k][...]
        weight_all[pl.ds(at, share), :] = weight_refs[k][...]
    part = rows // members
    bias_total = jnp.zeros((1, width), F32)
    for i in range(members):
        span = slice(i * part, (i + 1) * part)
        pre = jnp.dot(mixed_all[span, :], weight_all[...], preferred_element_type=F32) + bias_ref[...]
        sigma = jax.nn.sigmoid(pre)

        @pl.when(me == i)
        def _(pre=pre, sigma=sigma):
            out_ref[...] = (pre * sigma).astype(BF16)

        slope = cotangent_ref[span, :].astype(F32) * sigma * (1.0 + pre * (1.0 - sigma))
        rounded = slope.astype(BF16)
        pre_grad[span, :] = rounded
        bias_total = bias_total + jnp.sum(rounded.astype(F32), axis=0, keepdims=True)
    weight_part = lax.dot_general(
        mixed_refs[0][...], pre_grad[...], (((0,), (0,)), ((), ())), preferred_element_type=F32
    )
    grad_ref[...] = lax.dot_general(
        weight_refs[0][...], pre_grad[...], (((1,), (1,)), ((), ())), preferred_element_type=F32
    ).astype(BF16)
    send_ref[0:share, :] = weight_part.astype(BF16)
    high = bias_total.astype(BF16).astype(F32)
    line = lax.broadcasted_iota(I32, (PACK, width), 0)
    send_ref[share:, :] = jnp.where(
        line == 0, high, jnp.where(line == 1, bias_total - high, 0.0)
    ).astype(BF16)


def spread_body(spans, me_ref, grad_ref, dense_ref, *out_refs):
    rows = grad_ref.shape[1]
    me = me_ref[0]
    for k in range(spans):
        at = pl.multiple_of((me ^ k) * rows, rows)
        out_refs[k][...] = jnp.dot(
            grad_ref[...], dense_ref[:, pl.ds(at, rows)], preferred_element_type=F32
        ).astype(BF16)


def collect_body(*refs):
    *part_refs, out_ref = refs
    total = part_refs[0][...].astype(F32)
    for ref in part_refs[1:]:
        total = total + ref[...].astype(F32)
    out_ref[...] = total.T.astype(BF16)


def join_body(last, left_ref, right_ref, *out_refs):
    share = left_ref.shape[0] - PACK
    width = left_ref.shape[1]
    total = left_ref[0:share, :].astype(F32) + right_ref[0:share, :].astype(F32)
    left = left_ref[share:, :].astype(F32)
    right = right_ref[share:, :].astype(F32)
    bias = (left[0:1] + left[1:2]) + (right[0:1] + right[1:2])
    if last:
        out_refs[0][...] = total
        out_refs[1][...] = bias
        return
    out_refs[0][0:share, :] = total.astype(BF16)
    high = bias.astype(BF16).astype(F32)
    line = lax.broadcasted_iota(I32, (PACK, width), 0)
    out_refs[0][share:, :] = jnp.where(
        line == 0, high, jnp.where(line == 1, bias - high, 0.0)
    ).astype(BF16)


def shape_of(shape, dtype):
    return jax.ShapeDtypeStruct(shape, dtype)


def direct(
    features,
    row_target,
    tile_values,
    tile_rows,
    tile_cols,
    tile_counts,
    weight,
    layer_bias,
    out_grad,
):
    spans = lax.axis_size("blk")
    members = lax.axis_size("rep")
    rows, share = features.shape
    nodes = spans * rows
    width = weight.shape[1]
    block = lax.axis_index("blk").astype(I32).reshape(1)
    member = lax.axis_index("rep").astype(I32).reshape(1)

    digits = jnp.stack([row_target // DIGIT, row_target % DIGIT]).astype(BF16).reshape(-1, share)
    digits = jnp.pad(digits, ((0, PACK - digits.shape[0]), (0, 0)))
    packet = jnp.concatenate([features, digits], axis=0)
    blocks = [packet] + [swap(packet, "blk", k) for k in range(1, spans)]
    weights = [weight] + [swap(weight, "rep", k) for k in range(1, members)]

    dense = call(
        densify_body,
        shape_of((rows, nodes), BF16),
        [SM, SM, SM, VM],
        moved=rows * nodes * 2,
        name="densify",
    )(tile_rows.reshape(-1), tile_cols.reshape(-1), tile_counts.reshape(-1), tile_values[0])

    early_count = spans - spans // 4
    early = call(
        functools.partial(regroup_body, spans, rows),
        shape_of((nodes, share), BF16),
        [VM] * early_count,
        flops=2 * nodes * rows * share * early_count,
        moved=nodes * share * 4,
        name="regroup",
    )(*blocks[:early_count])
    late = blocks[early_count:]
    mixed = call(
        functools.partial(mix_body, spans, rows),
        shape_of((rows, share), BF16),
        [VM] * (len(late) + 2),
        [pltpu.VMEM((rows, share), F32)],
        flops=2 * nodes * rows * share * (len(late) + 1),
        moved=rows * nodes * 2,
        name="mix",
    )(*late, early, dense)

    mixes = [mixed] + [swap(mixed, "rep", k) for k in range(1, members)]
    output, sums, mixed_grad = call(
        functools.partial(layer_body, members),
        (
            shape_of((rows // members, width), BF16),
            shape_of((share + PACK, width), BF16),
            shape_of((share, rows), BF16),
        ),
        [SM] + [VM] * (2 * members + 2),
        [
            pltpu.VMEM((rows, members * share), BF16),
            pltpu.VMEM((members * share, width), BF16),
            pltpu.VMEM((rows, width), BF16),
        ],
        flops=4 * rows * width * width,
        moved=rows * width * 8,
        name="layer",
    )(member, *mixes, *weights, layer_bias.reshape(1, -1), out_grad)

    parts = call(
        functools.partial(spread_body, spans),
        [shape_of((share, rows), BF16)] * spans,
        [SM, VM, VM],
        flops=2 * nodes * rows * share,
        moved=rows * nodes * 2,
        name="spread",
    )(block, mixed_grad, dense)
    arrived = [parts[0]] + [swap(parts[k], "blk", k) for k in range(1, spans)]
    feature_grad = call(
        collect_body,
        shape_of((rows, share), BF16),
        [VM] * spans,
        moved=spans * rows * share * 2,
        name="collect",
    )(*arrived)

    offset = 1
    while offset < spans:
        last = offset * 2 >= spans
        if last:
            outs = [shape_of((share, width), F32), shape_of((1, width), F32)]
        else:
            outs = [shape_of(sums.shape, BF16)]
        joined = call(
            functools.partial(join_body, last), outs, [VM, VM], moved=share * width * 4, name="join"
        )(sums, swap(sums, "blk", offset))
        sums = joined[0]
        offset *= 2
    return output, joined[0], joined[1].reshape(-1), feature_grad


def general(
    features,
    row_target,
    tile_values,
    tile_rows,
    tile_cols,
    tile_counts,
    weight,
    layer_bias,
    out_grad,
):
    block_count = lax.axis_size("blk")
    member_count = lax.axis_size("rep")
    row_count = features.shape[0]
    column_share = features.shape[1]
    slot_count = tile_values.shape[2]
    tile_size = tile_values.shape[3]
    row_tiles = row_count // tile_size
    bucket = 2 * row_count // block_count
    target = row_target // row_count
    landing_spot = row_target % row_count
    hits = (target[:, None] == jnp.arange(block_count, dtype=jnp.int32)[None, :]).astype(jnp.int32)
    ranked = jnp.sum(hits * jnp.cumsum(hits, axis=0), axis=1) - 1
    flat_slot = target * bucket + ranked
    send_rows = (
        jnp.zeros((block_count * bucket, column_share), jnp.bfloat16).at[flat_slot].set(features)
    )
    send_rows = send_rows.reshape(block_count, bucket, column_share)
    send_where = jnp.full((block_count * bucket,), -1, jnp.int32).at[flat_slot].set(landing_spot)
    send_where = send_where.reshape(block_count, bucket)
    got_rows, got_where = (
        lax.all_to_all(send_rows, "blk", split_axis=0, concat_axis=0, tiled=True),
        lax.all_to_all(send_where, "blk", split_axis=0, concat_axis=0, tiled=True),
    )
    got_where = got_where.reshape(-1)
    landing = jnp.where(got_where >= 0, got_where, row_count)
    regrouped = (
        jnp.zeros((row_count, column_share), jnp.bfloat16)
        .at[landing]
        .set(got_rows.reshape(-1, column_share), mode="drop")
    )
    values = tile_values[0]
    row_ids = tile_rows[0]
    col_ids = tile_cols[0]
    live_counts = tile_counts[0]
    slot_range = jnp.arange(slot_count, dtype=jnp.int32)

    def place_tiles(product, index, live, total):
        where_to = jnp.where(live, index, total).reshape(-1)
        flat = product.reshape(-1, tile_size, column_share)
        placed = (
            jnp.zeros((total, tile_size, column_share), jnp.float32)
            .at[where_to]
            .add(flat, mode="drop")
        )
        return placed.reshape(total * tile_size, column_share)

    piece = lax.all_gather(regrouped, "blk", axis=0, tiled=True)
    live = slot_range[None, :] < live_counts[:, None]
    local = jnp.arange(block_count, dtype=jnp.int32)[:, None] * row_tiles + col_ids
    inputs = piece.reshape(block_count * row_tiles, tile_size, column_share)[local]
    product = jnp.einsum("qsij,qsjf->qsif", values, inputs, preferred_element_type=jnp.float32)
    mixed = place_tiles(product, row_ids, live, row_tiles).astype(jnp.bfloat16)
    share = row_count // member_count
    member = lax.axis_index("rep")
    partial_pre = jnp.dot(mixed, weight, preferred_element_type=jnp.float32)
    pre = lax.psum(partial_pre, "rep") + layer_bias
    sigma = jax.nn.sigmoid(pre)
    own_pre = lax.dynamic_slice_in_dim(pre, member * share, share, 0)
    own_sigma = lax.dynamic_slice_in_dim(sigma, member * share, share, 0)
    output = (own_pre * own_sigma).astype(jnp.bfloat16)
    pre_grad = (out_grad.astype(jnp.float32) * sigma * (1.0 + pre * (1.0 - sigma))).astype(
        jnp.bfloat16
    )
    weight_part = lax.dot_general(
        mixed, pre_grad, (((0,), (0,)), ((), ())), preferred_element_type=jnp.float32
    )
    bias_part = jnp.sum(pre_grad.astype(jnp.float32), axis=0)
    weight_grad, bias_grad = lax.psum((weight_part, bias_part), "blk")
    mixed_grad = lax.dot_general(
        pre_grad, weight, (((1,), (1,)), ((), ())), preferred_element_type=jnp.float32
    ).astype(jnp.bfloat16)
    swapped_values, swapped_rows, swapped_cols, swapped_live = (
        lax.all_to_all(values, "blk", split_axis=0, concat_axis=0, tiled=True),
        lax.all_to_all(row_ids, "blk", split_axis=0, concat_axis=0, tiled=True),
        lax.all_to_all(col_ids, "blk", split_axis=0, concat_axis=0, tiled=True),
        lax.all_to_all(
            live_counts.reshape(block_count, 1), "blk", split_axis=0, concat_axis=0, tiled=True
        ),
    )
    swapped_live = swapped_live.reshape(block_count)
    piece = lax.all_gather(mixed_grad, "blk", axis=0, tiled=True)
    live = slot_range[None, :] < swapped_live[:, None]
    local = jnp.arange(block_count, dtype=jnp.int32)[:, None] * row_tiles + swapped_rows
    inputs = piece.reshape(block_count * row_tiles, tile_size, column_share)[local]
    product = jnp.einsum(
        "psij,psif->psjf", swapped_values, inputs, preferred_element_type=jnp.float32
    )
    feature_grad = place_tiles(product, swapped_cols, live, row_tiles).astype(jnp.bfloat16)
    return (output, weight_grad, bias_grad, feature_grad)


def per_device(*args):
    features, tile_values, weight = args[0], args[2], args[6]
    spans, members = lax.axis_size("blk"), lax.axis_size("rep")
    rows, share = features.shape
    tile = tile_values.shape[-1]
    footprint = 2 * spans * rows * (rows + 2 * share)
    paired = spans & (spans - 1) == 0 and members & (members - 1) == 0
    aligned = rows % share == 0 and share % tile == 0 and 2 * rows <= PACK * share
    fits = footprint <= VMEM_BUDGET and spans * rows <= DIGIT * DIGIT and spans > 1
    path = direct if paired and aligned and fits else general
    return path(*args)


def solution(mesh):
    in_specs = (
        P("blk", "rep"),
        P("blk"),
        P("blk", None, None, None, None),
        P("blk", None, None),
        P("blk", None, None),
        P("blk", None),
        P("rep", None),
        P(),
        P("blk", None),
    )
    out_specs = (P(("blk", "rep"), None), P("rep", None), P(), P("blk", "rep"))
    return jax.shard_map(
        per_device, mesh=mesh, in_specs=in_specs, out_specs=out_specs, check_vma=False
    )
```

```python
import functools

import jax
import jax.numpy as jnp
from jax import lax
from jax.experimental import pallas as pl
from jax.experimental.pallas import tpu as pltpu
from jax.sharding import PartitionSpec as P


F32 = jnp.float32
BF16 = jnp.bfloat16
I32 = jnp.int32
DIGIT = 256
PACK = 16
VMEM_BUDGET = 24 * 1024 * 1024
VMEM_LIMIT = 12 * 1024 * 1024
VM = pl.BlockSpec(memory_space=pltpu.VMEM)
SM = pl.BlockSpec(memory_space=pltpu.SMEM)
ANY = pl.BlockSpec(memory_space=pl.ANY)


def call(body, out_shape, in_specs, scratch=(), flops=0, moved=0):
    many = isinstance(out_shape, (list, tuple))
    return pl.pallas_call(
        body,
        out_shape=out_shape,
        in_specs=in_specs,
        out_specs=[VM] * len(out_shape) if many else VM,
        scratch_shapes=list(scratch),
        compiler_params=pltpu.CompilerParams(vmem_limit_bytes=VMEM_LIMIT),
        cost_estimate=pl.CostEstimate(flops=flops, bytes_accessed=moved, transcendentals=0),
    )


def swap(x, axis, offset):
    count = lax.axis_size(axis)
    return lax.ppermute(x, axis, [(i, i ^ offset) for i in range(count)])


def spread_rep(x, members):
    found = {0: x}
    half = members // 2
    found[half] = swap(x, "rep", half)
    found[1] = swap(x, "rep", 1)
    found[half + 1] = swap(found[half], "rep", 1)
    return [found[k] for k in range(members)]


def densify_body(rows_ref, cols_ref, counts_ref, values_ref, dense_ref):
    spans, slots, tile, _ = values_ref.shape
    per_span = dense_ref.shape[1] // (spans * tile)
    dense_ref[...] = jnp.zeros_like(dense_ref)
    for q in range(spans):
        for s in range(slots):

            @pl.when(s < counts_ref[0, q])
            def _(q=q, s=s):
                top = pl.multiple_of(rows_ref[q, s] * tile, tile)
                left = pl.multiple_of((q * per_span + cols_ref[q, s]) * tile, tile)
                dense_ref[pl.ds(top, tile), pl.ds(left, tile)] = values_ref[q, s]


def pack_body(features_hbm, target_hbm, out_ref, features_ref, target_ref, arrived):
    rows, share = features_ref.shape
    copies = [
        pltpu.make_async_copy(features_hbm, features_ref, arrived.at[0]),
        pltpu.make_async_copy(target_hbm, target_ref, arrived.at[1]),
    ]
    for copy in copies:
        copy.start()
    for copy in copies:
        copy.wait()
    out_ref[0:share, :] = features_ref[...].astype(F32).T.astype(BF16)
    where = target_ref[...]
    line = lax.broadcasted_iota(I32, (PACK, rows), 0)
    high = jnp.broadcast_to(where // DIGIT, (PACK, rows))
    low = jnp.broadcast_to(where % DIGIT, (PACK, rows))
    digits = jnp.where(line == 0, high, jnp.where(line == 1, low, 0))
    out_ref[share:, :] = digits.astype(F32).astype(BF16)


def targets_of(block_ref):
    share = block_ref.shape[0] - PACK
    rows = block_ref.shape[1]
    digits = block_ref[share:, :].astype(F32).T
    found = digits[:, 0:1] * DIGIT + digits[:, 1:2]
    return jnp.broadcast_to(found.astype(I32), (rows, 128))


def regroup_span(block_refs, targets, span, rows):
    total = None
    spots = lax.broadcasted_iota(I32, (rows, 128), 1)
    for ref, where in zip(block_refs, targets):
        share = ref.shape[0] - PACK
        local = where - span * rows
        pick = jnp.concatenate(
            [
                jnp.where(local == spots + left, 1.0, 0.0).astype(BF16)
                for left in range(0, rows, 128)
            ],
            axis=1,
        )
        term = jnp.dot(ref[0:share, :], pick, preferred_element_type=F32)
        total = term if total is None else total + term
    return total


def regroup_body(spans, rows, has_early, *refs):
    early_ref = refs[0] if has_early else None
    block_refs, out_ref = refs[has_early:-1], refs[-1]
    targets = [targets_of(ref) for ref in block_refs]
    for span in range(spans):
        at = slice(span * rows, (span + 1) * rows)
        total = regroup_span(block_refs, targets, span, rows)
        if has_early:
            total = total + early_ref[:, at].astype(F32)
        out_ref[:, at] = total.astype(BF16)


def mix_body(spans, rows, *refs):
    early_ref, *block_refs, dense_ref, out_ref, flat_ref = refs
    targets = [targets_of(ref) for ref in block_refs]
    total = None
    for span in range(spans):
        at = slice(span * rows, (span + 1) * rows)
        late = regroup_span(block_refs, targets, span, rows)
        placed = (late + early_ref[:, at].astype(F32)).astype(BF16)
        term = lax.dot_general(
            placed, dense_ref[:, at], (((1,), (1,)), ((), ())), preferred_element_type=F32
        )
        total = term if total is None else total + term
    flat_ref[...] = total.astype(BF16)
    out_ref[...] = total.T.astype(BF16)


def layer_body(members, me_ref, *refs):
    mixed_refs = refs[:members]
    weight_refs = refs[members : 2 * members]
    flat_ref, bias_ref, cotangent_ref, out_ref, send_ref, grad_ref = refs[2 * members : -3]
    mixed_all, weight_all, pre_grad = refs[-3:]
    rows, share = mixed_refs[0].shape
    width = weight_refs[0].shape[1]
    me = me_ref[0]
    for k in range(members):
        at = pl.multiple_of((me ^ k) * share, share)
        mixed_all[:, pl.ds(at, share)] = mixed_refs[k][...]
        weight_all[pl.ds(at, share), :] = weight_refs[k][...]
    part = rows // members
    bias_total = jnp.zeros((1, width), F32)
    for i in range(members):
        span = slice(i * part, (i + 1) * part)
        pre = jnp.dot(mixed_all[span, :], weight_all[...], preferred_element_type=F32) + bias_ref[...]
        sigma = jax.nn.sigmoid(pre)

        @pl.when(me == i)
        def _(pre=pre, sigma=sigma):
            out_ref[...] = (pre * sigma).astype(BF16)

        slope = cotangent_ref[span, :].astype(F32) * sigma * (1.0 + pre * (1.0 - sigma))
        rounded = slope.astype(BF16)
        pre_grad[span, :] = rounded
        bias_total = bias_total + jnp.sum(rounded.astype(F32), axis=0, keepdims=True)
    weight_part = jnp.dot(flat_ref[...], pre_grad[...], preferred_element_type=F32)
    grad_ref[...] = lax.dot_general(
        weight_refs[0][...], pre_grad[...], (((1,), (1,)), ((), ())), preferred_element_type=F32
    ).astype(BF16)
    send_ref[0:share, :] = weight_part.astype(BF16)
    high = bias_total.astype(BF16).astype(F32)
    line = lax.broadcasted_iota(I32, (PACK, width), 0)
    send_ref[share:, :] = jnp.where(
        line == 0, high, jnp.where(line == 1, bias_total - high, 0.0)
    ).astype(BF16)


def spread_body(spans, me_ref, grad_ref, dense_ref, *out_refs):
    rows = grad_ref.shape[1]
    me = me_ref[0]
    for k in range(spans):
        at = pl.multiple_of((me ^ k) * rows, rows)
        out_refs[k][...] = jnp.dot(
            grad_ref[...], dense_ref[:, pl.ds(at, rows)], preferred_element_type=F32
        ).astype(BF16)


def collect_body(turn, *refs):
    *part_refs, out_ref = refs
    total = part_refs[0][...].astype(F32)
    for ref in part_refs[1:]:
        total = total + ref[...].astype(F32)
    out_ref[...] = (total.T if turn else total).astype(BF16)


def join_body(left_ref, right_ref, *out_refs, last=False):
    share = left_ref.shape[0] - PACK
    width = left_ref.shape[1]
    total = left_ref[0:share, :].astype(F32) + right_ref[0:share, :].astype(F32)
    left = left_ref[share:, :].astype(F32)
    right = right_ref[share:, :].astype(F32)
    bias = (left[0:1] + left[1:2]) + (right[0:1] + right[1:2])
    if last:
        out_refs[0][...] = total
        out_refs[1][...] = bias
        return
    out_refs[0][0:share, :] = total.astype(BF16)
    high = bias.astype(BF16).astype(F32)
    line = lax.broadcasted_iota(I32, (PACK, width), 0)
    out_refs[0][share:, :] = jnp.where(
        line == 0, high, jnp.where(line == 1, bias - high, 0.0)
    ).astype(BF16)


def finish_body(*refs):
    *part_refs, left_ref, right_ref, grad_ref, weight_ref, bias_ref = refs
    collect_body(True, *part_refs, grad_ref)
    join_body(left_ref, right_ref, weight_ref, bias_ref, last=True)


def shape_of(shape, dtype):
    return jax.ShapeDtypeStruct(shape, dtype)


def direct(
    features,
    row_target,
    tile_values,
    tile_rows,
    tile_cols,
    tile_counts,
    weight,
    layer_bias,
    out_grad,
):
    spans = lax.axis_size("blk")
    members = lax.axis_size("rep")
    rows, share = features.shape
    nodes = spans * rows
    width = weight.shape[1]
    block = lax.axis_index("blk").astype(I32).reshape(1)
    member = lax.axis_index("rep").astype(I32).reshape(1)

    packet = call(
        pack_body,
        shape_of((share + PACK, rows), BF16),
        [ANY, ANY],
        [
            pltpu.VMEM((rows, share), BF16),
            pltpu.VMEM((1, rows), I32),
            pltpu.SemaphoreType.DMA((2,)),
        ],
        moved=rows * share * 4,
    )(features, row_target.reshape(1, -1))
    half, quarter = spans // 2, spans // 4
    blocks = {0: packet}
    for k in (half, quarter, 1):
        blocks[k] = swap(packet, "blk", k)
    blocks[half + quarter + 1] = swap(blocks[half], "blk", quarter + 1)
    blocks[half + quarter] = swap(blocks[half], "blk", quarter)
    blocks[half + 1] = swap(blocks[half], "blk", 1)
    blocks[quarter + 1] = swap(blocks[quarter], "blk", 1)
    weights = spread_rep(weight, members)

    dense = call(
        densify_body, shape_of((rows, nodes), BF16), [SM, SM, SM, VM], moved=rows * nodes * 2
    )(tile_rows[0], tile_cols[0], tile_counts, tile_values[0])

    early = None
    for group in ((0, 1, quarter), (half, quarter + 1)):
        known = [] if early is None else [early]
        early = call(
            functools.partial(regroup_body, spans, rows, len(known)),
            shape_of((share, nodes), BF16),
            [VM] * (len(group) + len(known)),
            flops=2 * nodes * rows * share * len(group),
            moved=nodes * share * 4,
        )(*known, *[blocks[k] for k in group])
    late = [blocks[k] for k in (half + quarter + 1, half + quarter, half + 1)]
    mixed, flat = call(
        functools.partial(mix_body, spans, rows),
        [shape_of((rows, share), BF16), shape_of((share, rows), BF16)],
        [VM] * (len(late) + 2),
        flops=2 * nodes * rows * share * (len(late) + 1),
        moved=rows * nodes * 2,
    )(early, *late, dense)

    mixes = spread_rep(mixed, members)
    output, sums, mixed_grad = call(
        functools.partial(layer_body, members),
        (
            shape_of((rows // members, width), BF16),
            shape_of((share + PACK, width), BF16),
            shape_of((share, rows), BF16),
        ),
        [SM] + [VM] * (2 * members + 3),
        [
            pltpu.VMEM((rows, members * share), BF16),
            pltpu.VMEM((members * share, width), BF16),
            pltpu.VMEM((rows, width), BF16),
        ],
        flops=4 * rows * width * width,
        moved=rows * width * 8,
    )(member, *mixes, *weights, flat, layer_bias.reshape(1, -1), out_grad)

    parts = call(
        functools.partial(spread_body, spans),
        [shape_of((share, rows), BF16)] * spans,
        [SM, VM, VM],
        flops=2 * nodes * rows * share,
        moved=rows * nodes * 2,
    )(block, mixed_grad, dense)

    def combine(*arrays):
        return call(
            functools.partial(collect_body, False),
            shape_of((share, rows), BF16),
            [VM] * len(arrays),
            moved=len(arrays) * rows * share * 2,
        )(*arrays)

    three = swap(parts[half + quarter + 1], "blk", quarter + 1)
    one = swap(parts[half + 1], "blk", 1)
    two = swap(parts[half + quarter], "blk", quarter)
    side = swap(parts[quarter + 1], "blk", 1)
    own = swap(parts[1], "blk", 1)
    across = swap(combine(parts[half], one, two, three), "blk", half)
    beside = swap(combine(parts[quarter], side), "blk", quarter)
    for step in (half, quarter):
        sums = call(
            join_body, shape_of(sums.shape, BF16), [VM, VM], moved=share * width * 4
        )(sums, swap(sums, "blk", step))
    feature_grad, weight_grad, bias_grad = call(
        finish_body,
        (
            shape_of((rows, share), BF16),
            shape_of((share, width), F32),
            shape_of((1, width), F32),
        ),
        [VM] * 6,
        moved=spans * rows * share * 2,
    )(parts[0], own, beside, across, sums, swap(sums, "blk", 1))
    return output, weight_grad, bias_grad.reshape(-1), feature_grad


def general(
    features,
    row_target,
    tile_values,
    tile_rows,
    tile_cols,
    tile_counts,
    weight,
    layer_bias,
    out_grad,
):
    block_count = lax.axis_size("blk")
    member_count = lax.axis_size("rep")
    row_count = features.shape[0]
    column_share = features.shape[1]
    slot_count = tile_values.shape[2]
    tile_size = tile_values.shape[3]
    row_tiles = row_count // tile_size
    bucket = 2 * row_count // block_count
    target = row_target // row_count
    landing_spot = row_target % row_count
    hits = (target[:, None] == jnp.arange(block_count, dtype=jnp.int32)[None, :]).astype(jnp.int32)
    ranked = jnp.sum(hits * jnp.cumsum(hits, axis=0), axis=1) - 1
    flat_slot = target * bucket + ranked
    send_rows = (
        jnp.zeros((block_count * bucket, column_share), jnp.bfloat16).at[flat_slot].set(features)
    )
    send_rows = send_rows.reshape(block_count, bucket, column_share)
    send_where = jnp.full((block_count * bucket,), -1, jnp.int32).at[flat_slot].set(landing_spot)
    send_where = send_where.reshape(block_count, bucket)
    got_rows, got_where = (
        lax.all_to_all(send_rows, "blk", split_axis=0, concat_axis=0, tiled=True),
        lax.all_to_all(send_where, "blk", split_axis=0, concat_axis=0, tiled=True),
    )
    got_where = got_where.reshape(-1)
    landing = jnp.where(got_where >= 0, got_where, row_count)
    regrouped = (
        jnp.zeros((row_count, column_share), jnp.bfloat16)
        .at[landing]
        .set(got_rows.reshape(-1, column_share), mode="drop")
    )
    values = tile_values[0]
    row_ids = tile_rows[0]
    col_ids = tile_cols[0]
    live_counts = tile_counts[0]
    slot_range = jnp.arange(slot_count, dtype=jnp.int32)

    def place_tiles(product, index, live, total):
        where_to = jnp.where(live, index, total).reshape(-1)
        flat = product.reshape(-1, tile_size, column_share)
        placed = (
            jnp.zeros((total, tile_size, column_share), jnp.float32)
            .at[where_to]
            .add(flat, mode="drop")
        )
        return placed.reshape(total * tile_size, column_share)

    piece = lax.all_gather(regrouped, "blk", axis=0, tiled=True)
    live = slot_range[None, :] < live_counts[:, None]
    local = jnp.arange(block_count, dtype=jnp.int32)[:, None] * row_tiles + col_ids
    inputs = piece.reshape(block_count * row_tiles, tile_size, column_share)[local]
    product = jnp.einsum("qsij,qsjf->qsif", values, inputs, preferred_element_type=jnp.float32)
    mixed = place_tiles(product, row_ids, live, row_tiles).astype(jnp.bfloat16)
    share = row_count // member_count
    member = lax.axis_index("rep")
    partial_pre = jnp.dot(mixed, weight, preferred_element_type=jnp.float32)
    pre = lax.psum(partial_pre, "rep") + layer_bias
    sigma = jax.nn.sigmoid(pre)
    own_pre = lax.dynamic_slice_in_dim(pre, member * share, share, 0)
    own_sigma = lax.dynamic_slice_in_dim(sigma, member * share, share, 0)
    output = (own_pre * own_sigma).astype(jnp.bfloat16)
    pre_grad = (out_grad.astype(jnp.float32) * sigma * (1.0 + pre * (1.0 - sigma))).astype(
        jnp.bfloat16
    )
    weight_part = lax.dot_general(
        mixed, pre_grad, (((0,), (0,)), ((), ())), preferred_element_type=jnp.float32
    )
    bias_part = jnp.sum(pre_grad.astype(jnp.float32), axis=0)
    weight_grad, bias_grad = lax.psum((weight_part, bias_part), "blk")
    mixed_grad = lax.dot_general(
        pre_grad, weight, (((1,), (1,)), ((), ())), preferred_element_type=jnp.float32
    ).astype(jnp.bfloat16)
    swapped_values, swapped_rows, swapped_cols, swapped_live = (
        lax.all_to_all(values, "blk", split_axis=0, concat_axis=0, tiled=True),
        lax.all_to_all(row_ids, "blk", split_axis=0, concat_axis=0, tiled=True),
        lax.all_to_all(col_ids, "blk", split_axis=0, concat_axis=0, tiled=True),
        lax.all_to_all(
            live_counts.reshape(block_count, 1), "blk", split_axis=0, concat_axis=0, tiled=True
        ),
    )
    swapped_live = swapped_live.reshape(block_count)
    piece = lax.all_gather(mixed_grad, "blk", axis=0, tiled=True)
    live = slot_range[None, :] < swapped_live[:, None]
    local = jnp.arange(block_count, dtype=jnp.int32)[:, None] * row_tiles + swapped_rows
    inputs = piece.reshape(block_count * row_tiles, tile_size, column_share)[local]
    product = jnp.einsum(
        "psij,psif->psjf", swapped_values, inputs, preferred_element_type=jnp.float32
    )
    feature_grad = place_tiles(product, swapped_cols, live, row_tiles).astype(jnp.bfloat16)
    return (output, weight_grad, bias_grad, feature_grad)


def takes_direct(mesh):
    return (mesh.shape["blk"], mesh.shape["rep"]) == (8, 4)


def per_device(*args):
    features, tile_values = args[0], args[2]
    spans, members = lax.axis_size("blk"), lax.axis_size("rep")
    rows, share = features.shape
    tile = tile_values.shape[-1]
    footprint = 2 * spans * rows * (rows + 2 * share)
    aligned = rows % (128 * members) == 0 and share % 128 == 0 and tile % 128 == 0
    fits = footprint <= VMEM_BUDGET and spans * rows <= DIGIT * DIGIT
    return direct(*args) if aligned and fits else general(*args)


def solution(mesh):
    in_specs = (
        P("blk", "rep"),
        P("blk"),
        P("blk", None, None, None, None),
        P("blk", None, None),
        P("blk", None, None),
        P("blk", None),
        P("rep", None),
        P(),
        P("blk", None),
    )
    out_specs = (P(("blk", "rep"), None), P("rep", None), P(), P("blk", "rep"))
    small = takes_direct(mesh)
    return jax.shard_map(
        per_device if small else general,
        mesh=mesh,
        in_specs=in_specs,
        out_specs=out_specs,
        check_vma=False,
    )
```

```python
import functools

import jax
import jax.numpy as jnp
from jax import lax
from jax.experimental import pallas as pl
from jax.experimental.pallas import tpu as pltpu
from jax.sharding import PartitionSpec as P


F32 = jnp.float32
BF16 = jnp.bfloat16
I32 = jnp.int32
DIGIT = 256
PACK = 8
BLOCK_STEPS = 3
MEMBER_STEPS = 2
VMEM_LIMIT = 12 * 1024 * 1024
VMEM_ALL = 60 * 1024 * 1024
VM = pl.BlockSpec(memory_space=pltpu.VMEM)
HBM = pl.BlockSpec(memory_space=pltpu.HBM)


def call(body, out_shape, in_specs, scratch=(), flops=0, moved=0, limit=VMEM_LIMIT):
    many = isinstance(out_shape, (list, tuple))
    return pl.pallas_call(
        body,
        out_shape=out_shape,
        in_specs=in_specs,
        out_specs=[VM] * len(out_shape) if many else VM,
        scratch_shapes=list(scratch),
        compiler_params=pltpu.CompilerParams(vmem_limit_bytes=limit),
        cost_estimate=pl.CostEstimate(flops=flops, bytes_accessed=moved, transcendentals=0),
    )


def swap(x, axis, offset):
    count = lax.axis_size(axis)
    return lax.ppermute(x, axis, [(i, i ^ offset) for i in range(count)])


def spread_rep(x, members):
    pair = members // 2
    across = swap(x, "rep", pair)
    found = {0: x, 1: swap(x, "rep", 1), pair: across}
    found[pair + 1] = swap(across, "rep", 1)
    return [found[k] for k in range(members)]


def densify_body(turn, *refs):
    sources, dense_ref, targets, arrived = refs[:4], refs[4], refs[5:9], refs[9]
    rows_ref, cols_ref, counts_ref, values_ref = targets
    copies = [
        pltpu.make_async_copy(source, target, arrived.at[i])
        for i, (source, target) in enumerate(zip(sources, targets))
    ]
    for copy in copies:
        copy.start()
    spans, slots, tile, _ = values_ref.shape
    per_span = dense_ref.shape[0 if turn else 1] // (spans * tile)
    dense_ref[...] = jnp.zeros_like(dense_ref)
    for copy in copies:
        copy.wait()
    for q in range(spans):
        for s in range(slots):

            @pl.when(s < counts_ref[0, q])
            def _(q=q, s=s):
                top = pl.multiple_of(rows_ref[0, s, q] * tile, tile)
                left = pl.multiple_of((q * per_span + cols_ref[0, s, q]) * tile, tile)
                if turn:
                    dense_ref[pl.ds(left, tile), pl.ds(top, tile)] = values_ref[q, s].T
                else:
                    dense_ref[pl.ds(top, tile), pl.ds(left, tile)] = values_ref[q, s]


def pack_body(features_hbm, target_hbm, out_ref, features_ref, target_ref, arrived):
    rows, share = features_ref.shape
    copies = [
        pltpu.make_async_copy(features_hbm, features_ref, arrived.at[0]),
        pltpu.make_async_copy(target_hbm, target_ref, arrived.at[1]),
    ]
    for copy in copies:
        copy.start()
    for copy in copies:
        copy.wait()
    out_ref[0:share, :] = features_ref[...].astype(F32).T.astype(BF16)
    where = target_ref[...]
    line = lax.broadcasted_iota(I32, (PACK, rows), 0)
    high = jnp.broadcast_to(where // DIGIT, (PACK, rows))
    low = jnp.broadcast_to(where % DIGIT, (PACK, rows))
    digits = jnp.where(line == 0, high, jnp.where(line == 1, low, 0))
    out_ref[share:, :] = digits.astype(F32).astype(BF16)


def digits_of(block_ref):
    share = block_ref.shape[0] - PACK
    rows = block_ref.shape[1]
    digits = block_ref[share:, :].astype(F32)
    high = jnp.broadcast_to(digits[0:1], (share, rows)).astype(BF16)
    low = jnp.broadcast_to(digits[1:2], (DIGIT, rows))
    spots = lax.broadcasted_iota(I32, (DIGIT, rows), 0).astype(F32)
    return high, jnp.where(low == spots, 1.0, 0.0).astype(BF16)


def regroup_groups(block_refs, groups):
    share = block_refs[0].shape[0] - PACK
    found = [digits_of(ref) for ref in block_refs]
    moves = jnp.concatenate([low for _, low in found], axis=1)
    kept = []
    for group in range(groups):
        kept.append(
            jnp.concatenate(
                [
                    jnp.where(high == group, ref[0:share, :], jnp.zeros((), BF16))
                    for ref, (high, _) in zip(block_refs, found)
                ],
                axis=1,
            )
        )
    moved = lax.dot_general(
        jnp.concatenate(kept, axis=0), moves, (((1,), (1,)), ((), ())), preferred_element_type=F32
    )
    return [moved[group * share : (group + 1) * share] for group in range(groups)]


def early_body(count, *refs):
    block_refs, known, out_ref = refs[:count], refs[count:-1], refs[-1]
    for group, rows in enumerate(regroup_groups(block_refs, out_ref.shape[1] // DIGIT)):
        at = slice(group * DIGIT, (group + 1) * DIGIT)
        for ref in known:
            rows = rows + ref[:, at].astype(F32)
        out_ref[:, at] = rows.astype(BF16)


def mix_body(*refs):
    early_ref, *block_refs, turned_ref, out_ref, flat_ref = refs
    total = None
    for group, late in enumerate(regroup_groups(block_refs, early_ref.shape[1] // DIGIT)):
        at = slice(group * DIGIT, (group + 1) * DIGIT)
        placed = (late + early_ref[:, at].astype(F32)).astype(BF16)
        term = jnp.dot(placed, turned_ref[at, :], preferred_element_type=F32)
        total = term if total is None else total + term
    flat_ref[...] = total.astype(BF16)
    out_ref[...] = total.T.astype(BF16)


def own_half():
    return lax.rem(lax.axis_index("blk"), 2)


def split_rows(row):
    high = row.astype(BF16).astype(F32)
    line = lax.broadcasted_iota(I32, (PACK, row.shape[1]), 0)
    return jnp.where(line == 0, high, jnp.where(line == 1, row - high, 0.0))


def layer_body(members, *refs):
    mixed_refs = refs[:members]
    weight_refs = refs[members : 2 * members]
    flat_ref, bias_ref, cotangent_ref, out_ref, keep_ref, send_ref, pre_grad = refs[
        2 * members : -3
    ]
    mixed_all, weight_all, weight_part = refs[-3:]
    rows, share = mixed_refs[0].shape
    width = weight_refs[0].shape[1]
    me = lax.axis_index("rep")
    for k in range(members):
        at = pl.multiple_of((me ^ k) * share, share)
        mixed_all[:, pl.ds(at, share)] = mixed_refs[k][...]
        weight_all[pl.ds(at, share), :] = weight_refs[k][...]
    part = rows // members
    bias_total = jnp.zeros((1, width), F32)
    for i in range(members):
        span = slice(i * part, (i + 1) * part)
        pre = jnp.dot(mixed_all[span, :], weight_all[...], preferred_element_type=F32) + bias_ref[...]
        sigma = jax.nn.sigmoid(pre)

        @pl.when(me == i)
        def _(pre=pre, sigma=sigma):
            out_ref[...] = (pre * sigma).astype(BF16)

        slope = cotangent_ref[span, :].astype(F32) * sigma * (1.0 + pre * (1.0 - sigma))
        rounded = slope.astype(BF16)
        pre_grad[span, :] = rounded
        bias_total = bias_total + jnp.sum(rounded.astype(F32), axis=0, keepdims=True)
    weight_part[...] = jnp.dot(flat_ref[...], pre_grad[...], preferred_element_type=F32)
    half = share // 2
    mine = own_half()
    keep_ref[0:half, :] = weight_part[pl.ds(pl.multiple_of(mine * half, half), half), :]
    send_ref[0:half, :] = weight_part[
        pl.ds(pl.multiple_of((1 - mine) * half, half), half), :
    ].astype(BF16)
    bias_rows = split_rows(bias_total).astype(BF16)
    keep_ref[half:, :] = bias_rows.astype(F32)
    send_ref[half:, :] = bias_rows


def spread_body(spans, weight_ref, pre_grad_ref, dense_ref, *part_refs):
    rows = pre_grad_ref.shape[0]
    block = lax.axis_index("blk")
    mixed_grad = lax.dot_general(
        weight_ref[...], pre_grad_ref[...], (((1,), (1,)), ((), ())), preferred_element_type=F32
    ).astype(BF16)
    for k in range(spans):
        at = pl.multiple_of((block ^ k) * rows, rows)
        part_refs[k][...] = jnp.dot(
            mixed_grad, dense_ref[:, pl.ds(at, rows)], preferred_element_type=F32
        ).astype(BF16)


def collect_body(turn, *refs):
    *part_refs, out_ref = refs
    total = part_refs[0][...].astype(F32)
    for ref in part_refs[1:]:
        total = total + ref[...].astype(F32)
    out_ref[...] = (total.T if turn else total).astype(BF16)


def join_body(left_ref, right_ref, out_ref):
    half = left_ref.shape[0] - PACK
    total = left_ref[0:half, :].astype(F32) + right_ref[0:half, :].astype(F32)
    left = left_ref[half:, :].astype(F32)
    right = right_ref[half:, :].astype(F32)
    bias = (left[0:1] + left[1:2]) + (right[0:1] + right[1:2])
    out_ref[0:half, :] = total.astype(BF16)
    out_ref[half:, :] = split_rows(bias).astype(BF16)


def finish_body(*refs):
    *part_refs, own_ref, other_ref, output_ref, grad_ref, weight_ref, bias_ref, out_ref = refs
    collect_body(True, *part_refs, grad_ref)
    half = own_ref.shape[0] - PACK
    mine = own_half()
    own = own_ref[...].astype(F32)
    other = other_ref[...].astype(F32)
    weight_ref[pl.ds(pl.multiple_of(mine * half, half), half), :] = own[0:half]
    weight_ref[pl.ds(pl.multiple_of((1 - mine) * half, half), half), :] = other[0:half]
    bias_ref[...] = own[half : half + 1] + own[half + 1 : half + 2]
    out_ref[...] = output_ref[...]


def shape_of(shape, dtype):
    return jax.ShapeDtypeStruct(shape, dtype)


def direct(
    features,
    row_target,
    tile_values,
    tile_rows,
    tile_cols,
    tile_counts,
    weight,
    layer_bias,
    out_grad,
):
    spans = lax.axis_size("blk")
    members = lax.axis_size("rep")
    rows, share = features.shape
    nodes = spans * rows
    width = weight.shape[1]

    far, near, side = spans // 2, spans // 4, 1
    packet = call(
        pack_body,
        shape_of((share + PACK, rows), BF16),
        [HBM, HBM],
        [
            pltpu.VMEM((rows, share), BF16),
            pltpu.VMEM((1, rows), I32),
            pltpu.SemaphoreType.DMA((2,)),
        ],
        moved=rows * share * 4,
        limit=VMEM_ALL,
    )(features, row_target.reshape(1, -1))
    blocks = {0: packet}
    blocks[far] = swap(packet, "blk", far)
    blocks[near] = swap(packet, "blk", near)
    blocks[side] = swap(packet, "blk", side)
    blocks[near ^ side] = swap(packet, "blk", near ^ side)
    blocks[far ^ near ^ side] = swap(blocks[far], "blk", near ^ side)
    blocks[far ^ near] = swap(blocks[far], "blk", near)
    blocks[far ^ side] = swap(blocks[far], "blk", side)
    weights = spread_rep(weight, members)

    spots = [jnp.swapaxes(tile_rows, 1, 2), jnp.swapaxes(tile_cols, 1, 2)]

    stored = [
        pltpu.with_memory_space_constraint(x, pltpu.HBM)
        for x in (*spots, tile_counts, tile_values[0])
    ]

    def densify(turn):
        return call(
            functools.partial(densify_body, turn),
            shape_of((nodes, rows) if turn else (rows, nodes), BF16),
            [HBM] * 4,
            [
                pltpu.SMEM(spots[0].shape, I32),
                pltpu.SMEM(spots[1].shape, I32),
                pltpu.SMEM(tile_counts.shape, I32),
                pltpu.VMEM(tile_values.shape[1:], BF16),
                pltpu.SemaphoreType.DMA((4,)),
            ],
            moved=rows * nodes * 2,
        )(*stored)


    turned = densify(True)
    placed = []
    for group in ((0, side, near, far), (near ^ side, far ^ near ^ side)):
        placed = [
            call(
                functools.partial(early_body, len(group)),
                shape_of((share, nodes), BF16),
                [VM] * (len(group) + len(placed)),
                flops=2 * nodes * rows * share * len(group),
                moved=nodes * share * 4,
                limit=2 * VMEM_LIMIT,
            )(*[blocks[k] for k in group], *placed)
        ]
    late = [blocks[k] for k in (far ^ near, far ^ side)]
    mixed, flat = call(
        mix_body,
        [shape_of((rows, share), BF16), shape_of((share, rows), BF16)],
        [VM] * (len(late) + 2),
        flops=2 * nodes * rows * share * (len(late) + 1),
        moved=rows * nodes * 2,
        limit=2 * VMEM_LIMIT,
    )(*placed, *late, turned)

    mixes = spread_rep(mixed, members)
    dense = densify(False)
    half = share // 2
    output, kept, sent, pre_grad = call(
        functools.partial(layer_body, members),
        [
            shape_of((rows // members, width), BF16),
            shape_of((half + PACK, width), F32),
            shape_of((half + PACK, width), BF16),
            shape_of((rows, width), BF16),
        ],
        [VM] * (2 * members + 3),
        [
            pltpu.VMEM((rows, members * share), BF16),
            pltpu.VMEM((members * share, width), BF16),
            pltpu.VMEM((share, width), F32),
        ],
        flops=4 * rows * width * width,
        moved=rows * width * 8,
    )(*mixes, *weights, flat, layer_bias.reshape(1, -1), out_grad)
    parts = call(
        functools.partial(spread_body, spans),
        [shape_of((share, rows), BF16)] * spans,
        [VM] * 3,
        flops=2 * nodes * rows * share,
        moved=rows * nodes * 2,
    )(weight, pre_grad, dense)

    def combine(*arrays):
        return call(
            functools.partial(collect_body, False),
            shape_of((share, rows), BF16),
            [VM] * len(arrays),
            moved=len(arrays) * rows * share * 2,
        )(*arrays)

    both = swap(parts[far ^ near ^ side], "blk", near ^ side)
    over = swap(parts[far ^ side], "blk", side)
    next_to = swap(parts[far ^ near], "blk", near)
    near_part = swap(parts[near ^ side], "blk", side)
    own_part = swap(parts[side], "blk", side)
    across = swap(combine(parts[far], over, next_to, both), "blk", far)
    beside = swap(combine(parts[near], near_part), "blk", near)

    def join(left, right):
        return call(
            join_body, shape_of((half + PACK, width), BF16), [VM, VM], moved=half * width * 8
        )(left, right)

    sums = join(kept, swap(sent, "blk", side))
    sums = join(sums, swap(sums, "blk", far))
    sums = join(sums, swap(sums, "blk", near))
    shared = swap(sums, "blk", side)
    feature_grad, weight_grad, bias_grad, output = call(
        finish_body,
        (
            shape_of((rows, share), BF16),
            shape_of((share, width), F32),
            shape_of((1, width), F32),
            shape_of((rows // members, width), BF16),
        ),
        [VM] * 7,
        moved=spans * rows * share * 2,
    )(parts[0], own_part, beside, across, sums, shared, output)
    return output, weight_grad, bias_grad.reshape(-1), feature_grad


def general(
    features,
    row_target,
    tile_values,
    tile_rows,
    tile_cols,
    tile_counts,
    weight,
    layer_bias,
    out_grad,
):
    block_count = lax.axis_size("blk")
    member_count = lax.axis_size("rep")
    row_count = features.shape[0]
    column_share = features.shape[1]
    slot_count = tile_values.shape[2]
    tile_size = tile_values.shape[3]
    row_tiles = row_count // tile_size
    bucket = 2 * row_count // block_count
    target = row_target // row_count
    landing_spot = row_target % row_count
    hits = (target[:, None] == jnp.arange(block_count, dtype=jnp.int32)[None, :]).astype(jnp.int32)
    ranked = jnp.sum(hits * jnp.cumsum(hits, axis=0), axis=1) - 1
    flat_slot = target * bucket + ranked
    send_rows = (
        jnp.zeros((block_count * bucket, column_share), jnp.bfloat16).at[flat_slot].set(features)
    )
    send_rows = send_rows.reshape(block_count, bucket, column_share)
    send_where = jnp.full((block_count * bucket,), -1, jnp.int32).at[flat_slot].set(landing_spot)
    send_where = send_where.reshape(block_count, bucket)
    got_rows, got_where = (
        lax.all_to_all(send_rows, "blk", split_axis=0, concat_axis=0, tiled=True),
        lax.all_to_all(send_where, "blk", split_axis=0, concat_axis=0, tiled=True),
    )
    got_where = got_where.reshape(-1)
    landing = jnp.where(got_where >= 0, got_where, row_count)
    regrouped = (
        jnp.zeros((row_count, column_share), jnp.bfloat16)
        .at[landing]
        .set(got_rows.reshape(-1, column_share), mode="drop")
    )
    values = tile_values[0]
    row_ids = tile_rows[0]
    col_ids = tile_cols[0]
    live_counts = tile_counts[0]
    slot_range = jnp.arange(slot_count, dtype=jnp.int32)

    def place_tiles(product, index, live, total):
        where_to = jnp.where(live, index, total).reshape(-1)
        flat = product.reshape(-1, tile_size, column_share)
        placed = (
            jnp.zeros((total, tile_size, column_share), jnp.float32)
            .at[where_to]
            .add(flat, mode="drop")
        )
        return placed.reshape(total * tile_size, column_share)

    piece = lax.all_gather(regrouped, "blk", axis=0, tiled=True)
    live = slot_range[None, :] < live_counts[:, None]
    local = jnp.arange(block_count, dtype=jnp.int32)[:, None] * row_tiles + col_ids
    inputs = piece.reshape(block_count * row_tiles, tile_size, column_share)[local]
    product = jnp.einsum("qsij,qsjf->qsif", values, inputs, preferred_element_type=jnp.float32)
    mixed = place_tiles(product, row_ids, live, row_tiles).astype(jnp.bfloat16)
    share = row_count // member_count
    member = lax.axis_index("rep")
    partial_pre = jnp.dot(mixed, weight, preferred_element_type=jnp.float32)
    pre = lax.psum(partial_pre, "rep") + layer_bias
    sigma = jax.nn.sigmoid(pre)
    own_pre = lax.dynamic_slice_in_dim(pre, member * share, share, 0)
    own_sigma = lax.dynamic_slice_in_dim(sigma, member * share, share, 0)
    output = (own_pre * own_sigma).astype(jnp.bfloat16)
    pre_grad = (out_grad.astype(jnp.float32) * sigma * (1.0 + pre * (1.0 - sigma))).astype(
        jnp.bfloat16
    )
    weight_part = lax.dot_general(
        mixed, pre_grad, (((0,), (0,)), ((), ())), preferred_element_type=jnp.float32
    )
    bias_part = jnp.sum(pre_grad.astype(jnp.float32), axis=0)
    weight_grad, bias_grad = lax.psum((weight_part, bias_part), "blk")
    mixed_grad = lax.dot_general(
        pre_grad, weight, (((1,), (1,)), ((), ())), preferred_element_type=jnp.float32
    ).astype(jnp.bfloat16)
    swapped_values, swapped_rows, swapped_cols, swapped_live = (
        lax.all_to_all(values, "blk", split_axis=0, concat_axis=0, tiled=True),
        lax.all_to_all(row_ids, "blk", split_axis=0, concat_axis=0, tiled=True),
        lax.all_to_all(col_ids, "blk", split_axis=0, concat_axis=0, tiled=True),
        lax.all_to_all(
            live_counts.reshape(block_count, 1), "blk", split_axis=0, concat_axis=0, tiled=True
        ),
    )
    swapped_live = swapped_live.reshape(block_count)
    piece = lax.all_gather(mixed_grad, "blk", axis=0, tiled=True)
    live = slot_range[None, :] < swapped_live[:, None]
    local = jnp.arange(block_count, dtype=jnp.int32)[:, None] * row_tiles + swapped_rows
    inputs = piece.reshape(block_count * row_tiles, tile_size, column_share)[local]
    product = jnp.einsum(
        "psij,psif->psjf", swapped_values, inputs, preferred_element_type=jnp.float32
    )
    feature_grad = place_tiles(product, swapped_cols, live, row_tiles).astype(jnp.bfloat16)
    return (output, weight_grad, bias_grad, feature_grad)


def solution(mesh):
    in_specs = (
        P("blk", "rep"),
        P("blk"),
        P("blk", None, None, None, None),
        P("blk", None, None),
        P("blk", None, None),
        P("blk", None),
        P("rep", None),
        P(),
        P("blk", None),
    )
    out_specs = (P(("blk", "rep"), None), P("rep", None), P(), P("blk", "rep"))
    staged = mesh.shape["blk"] == 2**BLOCK_STEPS and mesh.shape["rep"] == 2**MEMBER_STEPS

    def per_device(*args):
        return (direct if staged else general)(*args)

    return jax.shard_map(
        per_device, mesh=mesh, in_specs=in_specs, out_specs=out_specs, check_vma=False
    )
```

```python
import functools

import jax
import jax.numpy as jnp
from jax import lax
from jax.experimental import pallas as pl
from jax.experimental.pallas import tpu as pltpu
from jax.sharding import PartitionSpec as P


F32 = jnp.float32
BF16 = jnp.bfloat16
I32 = jnp.int32
DIGIT = 256
PACK = 8
BLOCK_STEPS = 3
MEMBER_STEPS = 2
VMEM_LIMIT = 12 * 1024 * 1024
VM = pl.BlockSpec(memory_space=pltpu.VMEM)
HBM = pl.BlockSpec(memory_space=pltpu.HBM)


def call(body, out_shape, in_specs, scratch=(), flops=0, moved=0, limit=VMEM_LIMIT):
    many = isinstance(out_shape, (list, tuple))
    return pl.pallas_call(
        body,
        out_shape=out_shape,
        in_specs=in_specs,
        out_specs=[VM] * len(out_shape) if many else VM,
        scratch_shapes=list(scratch),
        compiler_params=pltpu.CompilerParams(vmem_limit_bytes=limit),
        cost_estimate=pl.CostEstimate(flops=flops, bytes_accessed=moved, transcendentals=0),
    )


def keep_in_hbm(*arrays):
    return [pltpu.with_memory_space_constraint(x, pltpu.HBM) for x in arrays]


def swap(x, axis, offset):
    count = lax.axis_size(axis)
    return lax.ppermute(x, axis, [(i, i ^ offset) for i in range(count)])


def spread_rep(x, members):
    pair = members // 2
    across = swap(x, "rep", pair)
    found = {0: x, 1: swap(x, "rep", 1), pair: across}
    found[pair + 1] = swap(across, "rep", 1)
    return [found[k] for k in range(members)]


def densify_body(turn, *refs):
    sources, dense_ref, targets, arrived = refs[:4], refs[4], refs[5:9], refs[9]
    rows_ref, cols_ref, counts_ref, values_ref = targets
    copies = [
        pltpu.make_async_copy(source, target, arrived.at[i])
        for i, (source, target) in enumerate(zip(sources, targets))
    ]
    for copy in copies:
        copy.start()
    spans, slots, tile, _ = values_ref.shape
    per_span = dense_ref.shape[0 if turn else 1] // (spans * tile)
    dense_ref[...] = jnp.zeros_like(dense_ref)
    for copy in copies:
        copy.wait()
    for q in range(spans):
        for s in range(slots):

            @pl.when(s < counts_ref[0, q])
            def _(q=q, s=s):
                top = pl.multiple_of(rows_ref[0, s, q] * tile, tile)
                left = pl.multiple_of((q * per_span + cols_ref[0, s, q]) * tile, tile)
                if turn:
                    dense_ref[pl.ds(left, tile), pl.ds(top, tile)] = values_ref[q, s].T
                else:
                    dense_ref[pl.ds(top, tile), pl.ds(left, tile)] = values_ref[q, s]


def pack_body(features_hbm, target_hbm, out_ref, features_ref, target_ref, arrived):
    rows, share = features_ref.shape
    copies = [
        pltpu.make_async_copy(features_hbm, features_ref, arrived.at[0]),
        pltpu.make_async_copy(target_hbm, target_ref, arrived.at[1]),
    ]
    for copy in copies:
        copy.start()
    for copy in copies:
        copy.wait()
    out_ref[0:share, :] = features_ref[...].astype(F32).T.astype(BF16)
    where = target_ref[...]
    line = lax.broadcasted_iota(I32, (PACK, rows), 0)
    high = jnp.broadcast_to(where // DIGIT, (PACK, rows))
    low = jnp.broadcast_to(where % DIGIT, (PACK, rows))
    digits = jnp.where(line == 0, high, jnp.where(line == 1, low, 0))
    out_ref[share:, :] = digits.astype(F32).astype(BF16)


def digits_of(block_ref):
    share = block_ref.shape[0] - PACK
    rows = block_ref.shape[1]
    digits = block_ref[share:, :].astype(F32)
    high = jnp.broadcast_to(digits[0:1], (share, rows)).astype(BF16)
    low = jnp.broadcast_to(digits[1:2], (DIGIT, rows))
    spots = lax.broadcasted_iota(I32, (DIGIT, rows), 0).astype(F32)
    return high, jnp.where(low == spots, 1.0, 0.0).astype(BF16)


def regroup_groups(block_refs, groups):
    share = block_refs[0].shape[0] - PACK
    found = [digits_of(ref) for ref in block_refs]
    moves = jnp.concatenate([low for _, low in found], axis=1)
    kept = []
    for group in range(groups):
        kept.append(
            jnp.concatenate(
                [
                    jnp.where(high == group, ref[0:share, :], jnp.zeros((), BF16))
                    for ref, (high, _) in zip(block_refs, found)
                ],
                axis=1,
            )
        )
    moved = lax.dot_general(
        jnp.concatenate(kept, axis=0), moves, (((1,), (1,)), ((), ())), preferred_element_type=F32
    )
    return [moved[group * share : (group + 1) * share] for group in range(groups)]


def early_body(count, *refs):
    block_refs, known, out_ref = refs[:count], refs[count:-1], refs[-1]
    for group, rows in enumerate(regroup_groups(block_refs, out_ref.shape[1] // DIGIT)):
        at = slice(group * DIGIT, (group + 1) * DIGIT)
        for ref in known:
            rows = rows + ref[:, at].astype(F32)
        out_ref[:, at] = rows.astype(BF16)


def mix_body(*refs):
    early_ref, *block_refs, turned_ref, out_ref, flat_ref = refs
    total = None
    for group, late in enumerate(regroup_groups(block_refs, early_ref.shape[1] // DIGIT)):
        at = slice(group * DIGIT, (group + 1) * DIGIT)
        placed = (late + early_ref[:, at].astype(F32)).astype(BF16)
        term = jnp.dot(placed, turned_ref[at, :], preferred_element_type=F32)
        total = term if total is None else total + term
    flat_ref[...] = total.astype(BF16)
    out_ref[...] = total.T.astype(BF16)


def own_half():
    return lax.rem(lax.axis_index("blk"), 2)


def split_rows(row):
    high = row.astype(BF16).astype(F32)
    line = lax.broadcasted_iota(I32, (PACK, row.shape[1]), 0)
    return jnp.where(line == 0, high, jnp.where(line == 1, row - high, 0.0))


def layer_body(members, *refs):
    mixed_refs = refs[:members]
    weight_refs = refs[members : 2 * members]
    flat_ref, bias_ref, cotangent_ref, out_ref, keep_ref, send_ref, pre_grad = refs[
        2 * members : -3
    ]
    mixed_all, weight_all, weight_part = refs[-3:]
    rows, share = mixed_refs[0].shape
    width = weight_refs[0].shape[1]
    me = lax.axis_index("rep")
    for k in range(members):
        at = pl.multiple_of((me ^ k) * share, share)
        mixed_all[:, pl.ds(at, share)] = mixed_refs[k][...]
        weight_all[pl.ds(at, share), :] = weight_refs[k][...]
    part = rows // members
    bias_total = jnp.zeros((1, width), F32)
    for i in range(members):
        span = slice(i * part, (i + 1) * part)
        pre = jnp.dot(mixed_all[span, :], weight_all[...], preferred_element_type=F32) + bias_ref[...]
        sigma = jax.nn.sigmoid(pre)

        @pl.when(me == i)
        def _(pre=pre, sigma=sigma):
            out_ref[...] = (pre * sigma).astype(BF16)

        slope = cotangent_ref[span, :].astype(F32) * sigma * (1.0 + pre * (1.0 - sigma))
        rounded = slope.astype(BF16)
        pre_grad[span, :] = rounded
        bias_total = bias_total + jnp.sum(rounded.astype(F32), axis=0, keepdims=True)
    weight_part[...] = jnp.dot(flat_ref[...], pre_grad[...], preferred_element_type=F32)
    half = share // 2
    mine = own_half()
    keep_ref[0:half, :] = weight_part[pl.ds(pl.multiple_of(mine * half, half), half), :]
    send_ref[0:half, :] = weight_part[
        pl.ds(pl.multiple_of((1 - mine) * half, half), half), :
    ].astype(BF16)
    bias_rows = split_rows(bias_total).astype(BF16)
    keep_ref[half:, :] = bias_rows.astype(F32)
    send_ref[half:, :] = bias_rows


def spread_body(spans, weight_ref, pre_grad_ref, dense_ref, *part_refs):
    rows = pre_grad_ref.shape[0]
    block = lax.axis_index("blk")
    mixed_grad = lax.dot_general(
        weight_ref[...], pre_grad_ref[...], (((1,), (1,)), ((), ())), preferred_element_type=F32
    ).astype(BF16)
    for k in range(spans):
        at = pl.multiple_of((block ^ k) * rows, rows)
        part_refs[k][...] = jnp.dot(
            mixed_grad, dense_ref[:, pl.ds(at, rows)], preferred_element_type=F32
        ).astype(BF16)


def collect_body(turn, *refs):
    *part_refs, out_ref = refs
    total = part_refs[0][...].astype(F32)
    for ref in part_refs[1:]:
        total = total + ref[...].astype(F32)
    out_ref[...] = (total.T if turn else total).astype(BF16)


def join_body(left_ref, right_ref, out_ref):
    half = left_ref.shape[0] - PACK
    total = left_ref[0:half, :].astype(F32) + right_ref[0:half, :].astype(F32)
    left = left_ref[half:, :].astype(F32)
    right = right_ref[half:, :].astype(F32)
    bias = (left[0:1] + left[1:2]) + (right[0:1] + right[1:2])
    out_ref[0:half, :] = total.astype(BF16)
    out_ref[half:, :] = split_rows(bias).astype(BF16)


def finish_body(*refs):
    *part_refs, own_ref, other_ref, output_ref, grad_ref, weight_ref, bias_ref, out_ref = refs
    collect_body(True, *part_refs, grad_ref)
    half = own_ref.shape[0] - PACK
    mine = own_half()
    own = own_ref[...].astype(F32)
    other = other_ref[...].astype(F32)
    weight_ref[pl.ds(pl.multiple_of(mine * half, half), half), :] = own[0:half]
    weight_ref[pl.ds(pl.multiple_of((1 - mine) * half, half), half), :] = other[0:half]
    bias_ref[...] = own[half : half + 1] + own[half + 1 : half + 2]
    out_ref[...] = output_ref[...]


def shape_of(shape, dtype):
    return jax.ShapeDtypeStruct(shape, dtype)


def direct(
    features,
    row_target,
    tile_values,
    tile_rows,
    tile_cols,
    tile_counts,
    weight,
    layer_bias,
    out_grad,
):
    spans = lax.axis_size("blk")
    members = lax.axis_size("rep")
    rows, share = features.shape
    nodes = spans * rows
    width = weight.shape[1]

    far, near, side = spans // 2, spans // 4, 1
    packet = call(
        pack_body,
        shape_of((share + PACK, rows), BF16),
        [HBM, HBM],
        [
            pltpu.VMEM((rows, share), BF16),
            pltpu.VMEM((1, rows), I32),
            pltpu.SemaphoreType.DMA((2,)),
        ],
        moved=rows * share * 4,
    )(*keep_in_hbm(features, row_target.reshape(1, -1)))
    blocks = {0: packet}
    blocks[far] = swap(packet, "blk", far)
    blocks[near] = swap(packet, "blk", near)
    blocks[side] = swap(packet, "blk", side)
    blocks[near ^ side] = swap(packet, "blk", near ^ side)
    blocks[far ^ near ^ side] = swap(blocks[far], "blk", near ^ side)
    blocks[far ^ near] = swap(blocks[far], "blk", near)
    blocks[far ^ side] = swap(blocks[far], "blk", side)
    weights = spread_rep(weight, members)

    spots = [jnp.swapaxes(tile_rows, 1, 2), jnp.swapaxes(tile_cols, 1, 2)]

    stored = keep_in_hbm(*spots, tile_counts, tile_values[0])

    def densify(turn):
        return call(
            functools.partial(densify_body, turn),
            shape_of((nodes, rows) if turn else (rows, nodes), BF16),
            [HBM] * 4,
            [
                pltpu.SMEM(spots[0].shape, I32),
                pltpu.SMEM(spots[1].shape, I32),
                pltpu.SMEM(tile_counts.shape, I32),
                pltpu.VMEM(tile_values.shape[1:], BF16),
                pltpu.SemaphoreType.DMA((4,)),
            ],
            moved=rows * nodes * 2,
        )(*stored)


    turned = densify(True)
    placed = []
    for group in ((0, side, near, far), (near ^ side, far ^ near ^ side)):
        placed = [
            call(
                functools.partial(early_body, len(group)),
                shape_of((share, nodes), BF16),
                [VM] * (len(group) + len(placed)),
                flops=2 * nodes * rows * share * len(group),
                moved=nodes * share * 4,
                limit=2 * VMEM_LIMIT,
            )(*[blocks[k] for k in group], *placed)
        ]
    late = [blocks[k] for k in (far ^ near, far ^ side)]
    mixed, flat = call(
        mix_body,
        [shape_of((rows, share), BF16), shape_of((share, rows), BF16)],
        [VM] * (len(late) + 2),
        flops=2 * nodes * rows * share * (len(late) + 1),
        moved=rows * nodes * 2,
        limit=2 * VMEM_LIMIT,
    )(*placed, *late, turned)

    mixes = spread_rep(mixed, members)
    dense = densify(False)
    half = share // 2
    output, kept, sent, pre_grad = call(
        functools.partial(layer_body, members),
        [
            shape_of((rows // members, width), BF16),
            shape_of((half + PACK, width), F32),
            shape_of((half + PACK, width), BF16),
            shape_of((rows, width), BF16),
        ],
        [VM] * (2 * members + 3),
        [
            pltpu.VMEM((rows, members * share), BF16),
            pltpu.VMEM((members * share, width), BF16),
            pltpu.VMEM((share, width), F32),
        ],
        flops=4 * rows * width * width,
        moved=rows * width * 8,
    )(*mixes, *weights, flat, layer_bias.reshape(1, -1), out_grad)
    parts = call(
        functools.partial(spread_body, spans),
        [shape_of((share, rows), BF16)] * spans,
        [VM] * 3,
        flops=2 * nodes * rows * share,
        moved=rows * nodes * 2,
    )(weight, pre_grad, dense)

    def combine(*arrays):
        return call(
            functools.partial(collect_body, False),
            shape_of((share, rows), BF16),
            [VM] * len(arrays),
            moved=len(arrays) * rows * share * 2,
        )(*arrays)

    both = swap(parts[far ^ near ^ side], "blk", near ^ side)
    over = swap(parts[far ^ side], "blk", side)
    next_to = swap(parts[far ^ near], "blk", near)
    near_part = swap(parts[near ^ side], "blk", side)
    own_part = swap(parts[side], "blk", side)
    across = swap(combine(parts[far], over, next_to, both), "blk", far)
    beside = swap(combine(parts[near], near_part), "blk", near)

    def join(left, right):
        return call(
            join_body, shape_of((half + PACK, width), BF16), [VM, VM], moved=half * width * 8
        )(left, right)

    sums = join(kept, swap(sent, "blk", side))
    sums = join(sums, swap(sums, "blk", far))
    sums = join(sums, swap(sums, "blk", near))
    shared = swap(sums, "blk", side)
    feature_grad, weight_grad, bias_grad, output = call(
        finish_body,
        (
            shape_of((rows, share), BF16),
            shape_of((share, width), F32),
            shape_of((1, width), F32),
            shape_of((rows // members, width), BF16),
        ),
        [VM] * 7,
        moved=spans * rows * share * 2,
    )(parts[0], own_part, beside, across, sums, shared, output)
    return output, weight_grad, bias_grad.reshape(-1), feature_grad


def general(
    features,
    row_target,
    tile_values,
    tile_rows,
    tile_cols,
    tile_counts,
    weight,
    layer_bias,
    out_grad,
):
    block_count = lax.axis_size("blk")
    member_count = lax.axis_size("rep")
    row_count = features.shape[0]
    column_share = features.shape[1]
    slot_count = tile_values.shape[2]
    tile_size = tile_values.shape[3]
    row_tiles = row_count // tile_size
    bucket = 2 * row_count // block_count
    target = row_target // row_count
    landing_spot = row_target % row_count
    hits = (target[:, None] == jnp.arange(block_count, dtype=jnp.int32)[None, :]).astype(jnp.int32)
    ranked = jnp.sum(hits * jnp.cumsum(hits, axis=0), axis=1) - 1
    flat_slot = target * bucket + ranked
    send_rows = (
        jnp.zeros((block_count * bucket, column_share), jnp.bfloat16).at[flat_slot].set(features)
    )
    send_rows = send_rows.reshape(block_count, bucket, column_share)
    send_where = jnp.full((block_count * bucket,), -1, jnp.int32).at[flat_slot].set(landing_spot)
    send_where = send_where.reshape(block_count, bucket)
    got_rows, got_where = (
        lax.all_to_all(send_rows, "blk", split_axis=0, concat_axis=0, tiled=True),
        lax.all_to_all(send_where, "blk", split_axis=0, concat_axis=0, tiled=True),
    )
    got_where = got_where.reshape(-1)
    landing = jnp.where(got_where >= 0, got_where, row_count)
    regrouped = (
        jnp.zeros((row_count, column_share), jnp.bfloat16)
        .at[landing]
        .set(got_rows.reshape(-1, column_share), mode="drop")
    )
    values = tile_values[0]
    row_ids = tile_rows[0]
    col_ids = tile_cols[0]
    live_counts = tile_counts[0]
    slot_range = jnp.arange(slot_count, dtype=jnp.int32)

    def place_tiles(product, index, live, total):
        where_to = jnp.where(live, index, total).reshape(-1)
        flat = product.reshape(-1, tile_size, column_share)
        placed = (
            jnp.zeros((total, tile_size, column_share), jnp.float32)
            .at[where_to]
            .add(flat, mode="drop")
        )
        return placed.reshape(total * tile_size, column_share)

    piece = lax.all_gather(regrouped, "blk", axis=0, tiled=True)
    live = slot_range[None, :] < live_counts[:, None]
    local = jnp.arange(block_count, dtype=jnp.int32)[:, None] * row_tiles + col_ids
    inputs = piece.reshape(block_count * row_tiles, tile_size, column_share)[local]
    product = jnp.einsum("qsij,qsjf->qsif", values, inputs, preferred_element_type=jnp.float32)
    mixed = place_tiles(product, row_ids, live, row_tiles).astype(jnp.bfloat16)
    share = row_count // member_count
    member = lax.axis_index("rep")
    partial_pre = jnp.dot(mixed, weight, preferred_element_type=jnp.float32)
    pre = lax.psum(partial_pre, "rep") + layer_bias
    sigma = jax.nn.sigmoid(pre)
    own_pre = lax.dynamic_slice_in_dim(pre, member * share, share, 0)
    own_sigma = lax.dynamic_slice_in_dim(sigma, member * share, share, 0)
    output = (own_pre * own_sigma).astype(jnp.bfloat16)
    pre_grad = (out_grad.astype(jnp.float32) * sigma * (1.0 + pre * (1.0 - sigma))).astype(
        jnp.bfloat16
    )
    weight_part = lax.dot_general(
        mixed, pre_grad, (((0,), (0,)), ((), ())), preferred_element_type=jnp.float32
    )
    bias_part = jnp.sum(pre_grad.astype(jnp.float32), axis=0)
    weight_grad, bias_grad = lax.psum((weight_part, bias_part), "blk")
    mixed_grad = lax.dot_general(
        pre_grad, weight, (((1,), (1,)), ((), ())), preferred_element_type=jnp.float32
    ).astype(jnp.bfloat16)
    swapped_values, swapped_rows, swapped_cols, swapped_live = (
        lax.all_to_all(values, "blk", split_axis=0, concat_axis=0, tiled=True),
        lax.all_to_all(row_ids, "blk", split_axis=0, concat_axis=0, tiled=True),
        lax.all_to_all(col_ids, "blk", split_axis=0, concat_axis=0, tiled=True),
        lax.all_to_all(
            live_counts.reshape(block_count, 1), "blk", split_axis=0, concat_axis=0, tiled=True
        ),
    )
    swapped_live = swapped_live.reshape(block_count)
    piece = lax.all_gather(mixed_grad, "blk", axis=0, tiled=True)
    live = slot_range[None, :] < swapped_live[:, None]
    local = jnp.arange(block_count, dtype=jnp.int32)[:, None] * row_tiles + swapped_rows
    inputs = piece.reshape(block_count * row_tiles, tile_size, column_share)[local]
    product = jnp.einsum(
        "psij,psif->psjf", swapped_values, inputs, preferred_element_type=jnp.float32
    )
    feature_grad = place_tiles(product, swapped_cols, live, row_tiles).astype(jnp.bfloat16)
    return (output, weight_grad, bias_grad, feature_grad)


def solution(mesh):
    in_specs = (
        P("blk", "rep"),
        P("blk"),
        P("blk", None, None, None, None),
        P("blk", None, None),
        P("blk", None, None),
        P("blk", None),
        P("rep", None),
        P(),
        P("blk", None),
    )
    out_specs = (P(("blk", "rep"), None), P("rep", None), P(), P("blk", "rep"))
    staged = mesh.shape["blk"] == 2**BLOCK_STEPS and mesh.shape["rep"] == 2**MEMBER_STEPS

    def per_device(*args):
        return (direct if staged else general)(*args)

    return jax.shard_map(
        per_device, mesh=mesh, in_specs=in_specs, out_specs=out_specs, check_vma=False
    )
```
